32 devices in a mesh: dp: 4 (over z), tile: 8 (over y, x, core).
Axes of the slice: x: 2, y: 2, z: 4, core: 2. Of those that a mesh axis runs over, the one named last changes fastest.
Arguments:
- sensitivity: bfloat16 [2048, 2, 128, 128], P('dp', None, 'tile'), may hold values from -6 to 6
- diffusivity: float32 [2, 128, 128], P(None, 'tile'), may hold values from 0.02 to 0.16
Outputs:
- smoothed: bfloat16 [2048, 2, 128, 128], P('dp', None, 'tile')
- gram_matrix: float32 [2048, 2048], P('dp', 'tile')
The draws below stay inside these ranges and needn't reach their ends.
All inputs are finite; a program needn't handle non-finite values.
Results may differ from the reference program's by a relative error of at most 0.014.
Values may be sent and summed in bfloat16 or wider, within the bound.
A program may use at most 128 MiB of HBM per device.

```python
import math
import jax
import jax.numpy as jnp
from jax import lax

ROWS_DEV = 512
LAYERS = 2
NY = 128
STEPS = 4
NX = 128
ROWS = 2048
N_DP = 4


def block_scale(key, dims, shards, least, top_value):
    factor_of, own = 1.0, jax.random.fold_in(key, 6)
    for axis_at, shards_of in shards:
        draws = jnp.exp(jax.random.uniform(jax.random.fold_in(own, axis_at), (shards_of,), jnp.float32, least / len(shards), top_value / len(shards)))
        factor_of = factor_of * jnp.repeat(draws, dims[axis_at] // shards_of).reshape([-1 if axis == axis_at else 1 for axis in range(len(dims))])
    return factor_of


def scatter_about(rng, dims, width, limit, pieces=(), dtype=jnp.bfloat16):
    level = block_scale(rng, dims, pieces, -0.22, 0.18) if pieces else 1.0
    entries = jax.random.normal(rng, dims, jnp.float32) * width * level
    return jnp.minimum(jnp.maximum(entries, -limit), limit).astype(dtype)


def setup_inputs(seed: int = 0) -> dict:
    arg_keys = jax.random.split(jax.random.key(seed), 3)
    return {
        "sensitivity": scatter_about(arg_keys[0], (ROWS, LAYERS, NX, NY), 1.0, 6.0, ((0, 4), (2, 8))),
        "diffusivity": jnp.clip(jnp.exp(math.log(0.16) - 2.0794415 * jax.random.uniform(arg_keys[1], (LAYERS, NX, NY), jnp.float32) ** block_scale(arg_keys[1], (LAYERS, NX, NY), ((1, 8),), -0.2, 0.2)), 0.02, 0.16),
    }


def relax_step(field, coeff):
    centre = field[:, :, 1:-1]
    coeff_mid = coeff[:, 1:-1]
    change = 0.5 * (coeff_mid + coeff[:, 2:]) * (field[:, :, 2:] - centre)
    change = change + 0.5 * (coeff_mid + coeff[:, :-2]) * (field[:, :, :-2] - centre)
    padded = jnp.pad(centre, ((0, 0), (1, 1), (0, 0), (0, 0)))
    coeff_pad = jnp.pad(coeff_mid, ((1, 1), (0, 0), (0, 0)))
    change = change + 0.5 * (coeff_mid + coeff_pad[2:]) * (padded[:, 2:] - centre)
    change = change + 0.5 * (coeff_mid + coeff_pad[:-2]) * (padded[:, :-2] - centre)
    padded = jnp.pad(centre, ((0, 0), (0, 0), (0, 0), (1, 1)))
    coeff_pad = jnp.pad(coeff_mid, ((0, 0), (0, 0), (1, 1)))
    change = change + 0.5 * (coeff_mid + coeff_pad[:, :, 2:]) * (padded[:, :, :, 2:] - centre)
    change = change + 0.5 * (coeff_mid + coeff_pad[:, :, :-2]) * (padded[:, :, :, :-2] - centre)
    return centre + change


def smooth_group(group, diffusivity):
    coeff = jnp.pad(diffusivity, ((0, 0), (1, 1), (0, 0)))
    field = group
    for step_index in range(STEPS):
        widened = jnp.pad(field.astype(jnp.float32), ((0, 0), (0, 0), (1, 1), (0, 0)))
        field = relax_step(widened, coeff).astype(jnp.bfloat16)
    return field


def reference(sensitivity, diffusivity):
    groups = sensitivity.reshape(N_DP, ROWS_DEV, LAYERS, NX, NY)
    smoothed = lax.map(lambda group: smooth_group(group, diffusivity), groups)
    smoothed = smoothed.reshape(ROWS, LAYERS, NX, NY)
    flat_sens = sensitivity.reshape(ROWS, LAYERS * NX * NY)
    flat_smooth = smoothed.reshape(ROWS, LAYERS * NX * NY)
    total = lax.dot_general(flat_sens, flat_smooth, (((1,), (1,)), ((), ())), preferred_element_type=jnp.float32)
    gram_matrix = total / (LAYERS * NX * NY)
    return smoothed, gram_matrix
```

```python
import jax
import jax.numpy as jnp
from jax import lax
from jax.experimental import pallas as pl
from jax.experimental.pallas import tpu as pltpu
from jax.sharding import PartitionSpec as P

STEPS = 4
HALF = 2
MESH = pl.DeviceIdType.MESH
F32 = jnp.float32
BF16 = jnp.bfloat16


def neighbours(block, dim, width, axis="tile"):
    count = lax.axis_size(axis)
    forward = [(i, i + 1) for i in range(count - 1)]
    backward = [(t, s) for s, t in forward]
    low = lax.ppermute(
        lax.slice_in_dim(block, block.shape[dim] - width, None, axis=dim), axis, forward
    )
    high = lax.ppermute(lax.slice_in_dim(block, 0, width, axis=dim), axis, backward)
    return low, high


def extended(block, dim, width):
    low, high = neighbours(block, dim, width)
    return jnp.concatenate([low, block, high], axis=dim)


def coefficients(diffusivity):
    layers, width, ny = diffusivity.shape
    d = extended(diffusivity, 1, HALF)
    tile, tiles = lax.axis_index("tile"), lax.axis_size("tile")
    c = d[:, 1:-1]
    xm = 0.5 * (c + d[:, :-2])
    xp = 0.5 * (c + d[:, 2:])
    cp = jnp.pad(c, ((1, 1), (0, 0), (0, 0)))
    lm = 0.5 * (c + cp[:-2])
    lp = 0.5 * (c + cp[2:])
    cy = jnp.pad(c, ((0, 0), (0, 0), (1, 1)))
    ym = 0.5 * (c + cy[:, :, :-2])
    yp = 0.5 * (c + cy[:, :, 2:])
    a0 = 1.0 - (xm + xp + lm + lp + ym + yp)
    lay = jnp.arange(layers)[:, None, None]
    col = jnp.arange(ny)[None, None, :]
    other = jnp.where(lay == 0, lp, lm)
    ym = jnp.where(col == 0, 0.0, ym)
    yp = jnp.where(col == ny - 1, 0.0, yp)
    x = jnp.arange(width + 2)[None, :, None]
    inside = ((x > 0) | (tile > 0)) & ((x < width + 1) | (tile < tiles - 1))
    stack = jnp.where(inside[None], jnp.stack([a0, xm, xp, other, ym, yp]), 0.0)
    return stack.reshape(6, layers * (width + 2), ny)


def smooth_kernel(width, split, main_ref, low_ref, high_ref, coeff_ref, out_ref, *halves):
    lanes = 128
    half = width * lanes

    def load(layer, x):
        if x < HALF:
            at = (layer * HALF + x) * lanes
            return low_ref[:, at : at + lanes].astype(F32)
        if x >= width + HALF:
            at = (layer * HALF + x - width - HALF) * lanes
            return high_ref[:, at : at + lanes].astype(F32)
        at = (layer * width + x - HALF) * lanes
        return main_ref[:, at : at + lanes].astype(F32)

    def step(read, layer, x, cx):
        at = layer * (width + 2) + cx
        w = [coeff_ref[i, at : at + 1, :] for i in range(6)]
        f = read(layer, x)
        total = w[0] * f + w[1] * read(layer, x - 1) + w[2] * read(layer, x + 1)
        total = total + w[3] * read(1 - layer, x)
        total = total + w[4] * pltpu.roll(f, 1, 1)
        return total + w[5] * pltpu.roll(f, lanes - 1, 1)

    first = {}

    def read_first(layer, x):
        if (layer, x) not in first:
            first[layer, x] = step(load, layer, x, x - 1)
        return first[layer, x]

    for x in range(HALF, width + HALF):
        for layer in range(2):
            value = step(read_first, layer, x, x - 1)
            at = (layer * width + x - HALF) * lanes
            out_ref[:, at : at + lanes] = value.astype(BF16)
    if split:
        away_ref, keep_ref = halves
        left = 2 * lax.axis_index("dp") < lax.axis_size("dp")

        @pl.when(left)
        def _():
            away_ref[...] = out_ref[:, :half]
            keep_ref[...] = out_ref[:, half:]

        @pl.when(jnp.logical_not(left))
        def _():
            away_ref[...] = out_ref[:, half:]
            keep_ref[...] = out_ref[:, :half]


def two_steps(main, low, high, coeff, width, split):
    rows, cells = main.shape
    block = 32
    outs = [cells] + ([cells // 2] * 2 if split else [])
    return pl.pallas_call(
        lambda *refs: smooth_kernel(width, split, *refs),
        out_shape=[jax.ShapeDtypeStruct((rows, n), BF16) for n in outs],
        grid=(rows // block,),
        in_specs=[
            pl.BlockSpec((block, cells), lambda i: (i, 0)),
            pl.BlockSpec((block, low.shape[1]), lambda i: (i, 0)),
            pl.BlockSpec((block, high.shape[1]), lambda i: (i, 0)),
            pl.BlockSpec(coeff.shape, lambda i: (0, 0, 0)),
        ],
        out_specs=[pl.BlockSpec((block, n), lambda i: (i, 0)) for n in outs],
        cost_estimate=pl.CostEstimate(
            flops=rows * cells * 24, bytes_accessed=rows * cells * 8, transcendentals=0
        ),
        name="two_steps",
    )(main, low, high, coeff)


def exchange(tops, bottoms):
    count = lax.axis_size("tile")
    forward = [(i, i + 1) for i in range(count - 1)]
    low = lax.ppermute(tops, "tile", forward)
    high = lax.ppermute(bottoms, "tile", [(t, s) for s, t in forward])
    return low, high


def flat_halo(flat, width):
    n = width * 128
    w = HALF * 128
    tops = jnp.concatenate([flat[:, n - w : n], flat[:, 2 * n - w :]], axis=1)
    bottoms = jnp.concatenate([flat[:, :w], flat[:, n : n + w]], axis=1)
    return exchange(tops, bottoms)


def first_halo(block):
    rows, width = block.shape[0], block.shape[2]
    return exchange(
        block[:, :, width - HALF :].reshape(rows, -1), block[:, :, :HALF].reshape(rows, -1)
    )


def gram_dot(a, b):
    return lax.dot_general(a, b, (((1,), (1,)), ((), ())), preferred_element_type=F32)


def mix(width, load, store, coeff_ref):
    lanes = 128
    loaded, first = {}, {}

    def read(layer, x):
        if (layer, x) not in loaded:
            loaded[layer, x] = load(layer, x)
        return loaded[layer, x]

    def step(source, layer, x, cx):
        w = [coeff_ref[i, layer, cx : cx + 1, :] for i in range(6)]
        f = source(layer, x)
        total = w[0] * f + w[1] * source(layer, x - 1) + w[2] * source(layer, x + 1)
        total = total + w[3] * source(1 - layer, x)
        total = total + w[4] * pltpu.roll(f, 1, 1)
        return total + w[5] * pltpu.roll(f, lanes - 1, 1)

    def read_first(layer, x):
        if (layer, x) not in first:
            first[layer, x] = step(read, layer, x, x - 1)
        return first[layer, x]

    for x in range(HALF, width + HALF):
        for layer in range(2):
            store(layer, x - HALF, step(read_first, layer, x, x - 1))


def make_coefficients(tile, tiles, width, ny, d_ref, low_ref, high_ref, ext_ref, coeff_ref):
    base = 8
    for layer in range(2):
        ext_ref[layer, base : base + width, :] = d_ref[layer]

        @pl.when(tile > 0)
        def _():
            ext_ref[layer, base - HALF : base, :] = low_ref[layer, width - HALF : width, :]

        @pl.when(tile == 0)
        def _():
            ext_ref[layer, base - HALF : base, :] = jnp.zeros((HALF, ny), F32)

        @pl.when(tile < tiles - 1)
        def _():
            ext_ref[layer, base + width : base + width + HALF, :] = high_ref[layer, 0:HALF, :]

        @pl.when(tile == tiles - 1)
        def _():
            ext_ref[layer, base + width : base + width + HALF, :] = jnp.zeros((HALF, ny), F32)

    n = width + 2
    at = base - 1
    row = lax.broadcasted_iota(jnp.int32, (n, ny), 0)
    col = lax.broadcasted_iota(jnp.int32, (n, ny), 1)
    inside = ((row > 0) | (tile > 0)) & ((row < n - 1) | (tile < tiles - 1))
    for layer in range(2):
        c = ext_ref[layer, at : at + n, :]
        xm = 0.5 * (c + ext_ref[layer, at - 1 : at - 1 + n, :])
        xp = 0.5 * (c + ext_ref[layer, at + 1 : at + 1 + n, :])
        other = 0.5 * (c + ext_ref[1 - layer, at : at + n, :])
        ym = 0.5 * (c + jnp.where(col == 0, 0.0, pltpu.roll(c, 1, 1)))
        yp = 0.5 * (c + jnp.where(col == ny - 1, 0.0, pltpu.roll(c, ny - 1, 1)))
        a0 = 1.0 - (xm + xp + other + 0.5 * c + ym + yp)
        ym = jnp.where(col == 0, 0.0, ym)
        yp = jnp.where(col == ny - 1, 0.0, yp)
        for i, value in enumerate([a0, xm, xp, other, ym, yp]):
            coeff_ref[i, layer, 0:n, :] = jnp.where(inside, value, 0.0)


CHUNKS = 4
BLOCK = 32


def slab_kernel(scale, s_ref, d_ref, smoothed_ref, gram_ref, *scratch):
    (s32, m, native, mixed, near_away, near_keep, far_in, far_out, s_out, s_halo, m_halo,
     d_halo, d_ext, coeff, outgoing, own, partner, half_out, quarter, direct_out, turned_out,
     direct, turned, dif_send, dif_recv, sh_send, sh_recv, mh_send, mh_recv, aw_send, aw_recv,
     kp_send, kp_recv, fi_send, fi_recv, fo_send, fo_recv, out_sem,
     s1_send, s1_recv, s2_send, s2_recv, d_send, t_send, d_recv, t_recv) = scratch
    rows, width, ny = s_ref.shape[0], s_ref.shape[2], s_ref.shape[3]
    per = rows // CHUNKS
    p = lax.axis_index("dp")
    t = lax.axis_index("tile")
    tiles = 8
    u, v = t // 2, t % 2
    inner = (p == 1) | (p == 2)
    outer = jnp.logical_not(inner)
    away = jnp.where(p < 2, 0, 1)
    keep = 1 - away
    outer_of = jnp.where(p < 2, 0, 3)
    inner_of = jnp.where(p < 2, 1, 2)
    far_in_of = 3 - inner_of
    far_out_of = 3 - outer_of

    barrier = pltpu.get_barrier_semaphore()

    def greet(n, _):
        @pl.when(n != p * tiles + t)
        def _():
            pl.semaphore_signal(barrier, inc=1, device_id=(n // tiles, n % tiles), device_id_type=MESH)
        return 0

    lax.fori_loop(0, 32, greet, 0)
    pl.semaphore_wait(barrier, 31)

    def remote(src, dst, send, recv, to):
        return pltpu.make_async_remote_copy(
            src_ref=src, dst_ref=dst, send_sem=send, recv_sem=recv, device_id=to,
            device_id_type=MESH)

    sides = [(0, t < tiles - 1, t > 0, t + 1), (1, t > 0, t < tiles - 1, t - 1)]

    def dif_copy(side, to):
        return remote(d_ref, d_halo.at[side], dif_send.at[side], dif_recv.at[side], (p, to))

    def s_copy(side, to, c):
        at = pl.ds(c * per, per)
        return remote(s_out.at[side, at, :], s_halo.at[side, at, :], sh_send.at[side, c],
                      sh_recv.at[side, c], (p, to))

    def m_copy(side, to, c):
        at = pl.ds(c * per, per)
        w = HALF * ny
        cols = pl.ds(width * ny - w, w) if side == 0 else pl.ds(0, w)
        return remote(m.at[:, at, cols], m_halo.at[side, :, at, :], mh_send.at[side, c],
                      mh_recv.at[side, c], (p, to))

    for side, sends, _, to in sides:
        pl.when(sends)(lambda side=side, to=to: dif_copy(side, to).start())

    for c in range(CHUNKS):
        def unpack(i, _):
            i = c * (per // BLOCK) + i
            at = pl.ds(pl.multiple_of(i * BLOCK, BLOCK), BLOCK)
            for layer in range(2):
                value = s_ref[at, layer].astype(F32)
                s32[layer, pl.ds(pl.multiple_of(i * BLOCK * width, BLOCK * width), BLOCK * width), :] = (
                    value.reshape(BLOCK * width, ny))
                for h in range(HALF):
                    for side, x in ((0, width - HALF + h), (1, h)):
                        cols = slice((layer * HALF + h) * ny, (layer * HALF + h + 1) * ny)
                        s_out[side, at, cols] = s32[
                            layer, pl.ds(i * BLOCK * width + x, BLOCK, stride=width), :].astype(BF16)
            return 0

        lax.fori_loop(0, per // BLOCK, unpack, 0)
        for side, sends, _, to in sides:
            pl.when(sends)(lambda side=side, to=to, c=c: s_copy(side, to, c).start())

    for side, sends, gets, to in sides:
        @pl.when(gets)
        def _():
            dif_copy(side, to).wait_recv()

        @pl.when(jnp.logical_not(gets))
        def _():
            s_halo[side] = jnp.zeros(s_halo.shape[1:], BF16)
            m_halo[side] = jnp.zeros(m_halo.shape[1:], BF16)

    make_coefficients(t, tiles, width, ny, d_ref, d_halo.at[0], d_halo.at[1], d_ext, coeff)

    def chunk(ref, c):
        return ref.at[pl.ds(c * per, per), :]

    def own_away(c):
        return m.at[away, pl.ds(c * per, per), :]

    def away_copy(c):
        return remote(own_away(c), chunk(near_away, c), aw_send.at[c], aw_recv.at[c], (inner_of, t))

    def keep_copy(c):
        return remote(m.at[keep, pl.ds(c * per, per), :], chunk(near_keep, c), kp_send.at[c],
                      kp_recv.at[c], (inner_of, t))

    def in_copy(c):
        return remote(own_away(c), chunk(far_in, c), fi_send.at[c], fi_recv.at[c], (far_in_of, t))

    def out_copy(c):
        return remote(chunk(near_away, c), chunk(far_out, c), fo_send.at[c], fo_recv.at[c], (far_in_of, t))

    for c in range(CHUNKS):
        for side, _, gets, to in sides:
            pl.when(gets)(lambda side=side, to=to, c=c: s_copy(side, to, c).wait_recv())

        def first_half(i, _):
            i = c * (per // BLOCK) + i
            at = pl.ds(pl.multiple_of(i * BLOCK, BLOCK), BLOCK)

            def load(layer, x):
                if HALF <= x < width + HALF:
                    return s32[layer, pl.ds(i * BLOCK * width + x - HALF, BLOCK, stride=width), :]
                side, h = (0, x) if x < HALF else (1, x - width - HALF)
                cols = slice((layer * HALF + h) * ny, (layer * HALF + h + 1) * ny)
                return s_halo[side, at, cols].astype(F32)

            def store(layer, x, value):
                m[layer, at, x * ny : (x + 1) * ny] = value.astype(BF16)

            mix(width, load, store, coeff)
            return 0

        lax.fori_loop(0, per // BLOCK, first_half, 0)
        for side, sends, _, to in sides:
            pl.when(sends)(lambda side=side, to=to, c=c: m_copy(side, to, c).start())
        pl.when(inner)(lambda c=c: in_copy(c).start())
        pl.when(outer)(lambda c=c: away_copy(c).start())

    for c in range(CHUNKS):
        for side, _, gets, to in sides:
            pl.when(gets)(lambda side=side, to=to, c=c: m_copy(side, to, c).wait_recv())

        def second_half(i, _):
            i = c * (per // BLOCK) + i
            at = pl.ds(pl.multiple_of(i * BLOCK, BLOCK), BLOCK)

            def load(layer, x):
                if HALF <= x < width + HALF:
                    return m[layer, at, (x - HALF) * ny : (x - HALF + 1) * ny].astype(F32)
                side, h = (0, x) if x < HALF else (1, x - width - HALF)
                return m_halo[side, layer, at, h * ny : (h + 1) * ny].astype(F32)

            def store(layer, x, value):
                mixed[layer, pl.ds(x, BLOCK, stride=width), :] = value

            mix(width, load, store, coeff)
            for layer in range(2):
                native[at, layer] = mixed[layer].reshape(BLOCK, width, ny).astype(BF16)
            return 0

        lax.fori_loop(0, per // BLOCK, second_half, 0)
    write_out = pltpu.make_async_copy(native, smoothed_ref, out_sem.at[0])
    write_out.start()

    @pl.when(inner)
    def _():
        for c in range(CHUNKS):
            away_copy(c).wait_recv()
            out_copy(c).start()

    @pl.when(outer)
    def _():
        for c in range(CHUNKS):
            if c + 2 < CHUNKS:
                away_copy(c + 2).wait_send()
            else:
                keep_copy(c + 2 - CHUNKS).wait_send()
            keep_copy(c).start()

    def product(b, cols):
        if b == 5:
            return gram_dot(m[0], m[0, cols, :]) + gram_dot(m[1], m[1, cols, :])
        if b == 0:
            return gram_dot(near_away[...], m[away, cols, :]) + gram_dot(near_keep[...], m[keep, cols, :])
        if b == 1:
            return gram_dot(m[keep], far_in[cols, :])
        if b == 2:
            return gram_dot(m[keep], far_out[cols, :])
        return gram_dot(near_keep[...], (far_in if b == 3 else far_out)[cols, :])

    def when_active(b, run):
        if b == 5:
            run()
        else:
            pl.when(inner)(run)

    own_cols = pl.ds(pl.multiple_of(v * 256, 256), 256)
    other_cols = pl.ds(pl.multiple_of((1 - v) * 256, 256), 256)
    own_rows = pl.ds(pl.multiple_of(u * 128, 128), 128)

    def stage1(b):
        return remote(outgoing.at[b], partner.at[b], s1_send.at[b], s1_recv.at[b], (p, 2 * u + 1 - v))

    def stage2(b, k):
        to = (u + k) % 4
        return remote(
            half_out.at[b, pl.ds(pl.multiple_of(to * 128, 128), 128), :],
            quarter.at[b, k - 1], s2_send.at[b, k - 1], s2_recv.at[b, k - 1], (p, 2 * to + v))

    rows_of = [outer_of, inner_of, inner_of, outer_of, outer_of, p]
    cols_of = [inner_of, far_in_of, far_out_of, far_in_of, far_out_of, p]

    def send_direct(b, action):
        dp, dt = rows_of[b], 2 * cols_of[b] + v
        active = inner if b < 5 else (p >= 0)
        mine = (dp == p) & (dt == t)
        where = direct.at[pl.ds(pl.multiple_of(u * 128, 128), 128), :]
        copy = remote(direct_out.at[b], where, d_send.at[b], d_recv.at[u], (dp, dt))

        @pl.when(active & jnp.logical_not(mine))
        def _():
            copy.start() if action == 0 else copy.wait_send()

        if action == 0:
            @pl.when(active & mine)
            def _():
                where[...] = direct_out[b]

    def send_turned(b, action):
        dp, dt = cols_of[b], 2 * rows_of[b] + u // 2
        mine = (dp == p) & (dt == t)
        slot = v * 2 + u % 2
        copy = remote(turned_out.at[b], turned.at[slot], t_send.at[b], t_recv.at[slot], (dp, dt))

        @pl.when(inner & jnp.logical_not(mine))
        def _():
            copy.start() if action == 0 else copy.wait_send()

        if action == 0:
            @pl.when(inner & mine)
            def _():
                turned[slot] = turned_out[b]

    def reduce_blocks(order):
        for b in order:
            def begin(b=b):
                outgoing[b] = product(b, other_cols).astype(BF16)
                stage1(b).start()
            when_active(b, begin)
        for b in order:
            def add_partner(b=b):
                own[b] = product(b, own_cols)
                stage1(b).wait_recv()
                half_out[b] = (own[b] + partner[b].astype(F32)).astype(BF16)
                for k in range(1, 4):
                    stage2(b, k).start()
            when_active(b, add_partner)
        for b in order:
            def finish(b=b):
                value = own[b, own_rows, :] + partner[b, own_rows, :].astype(F32)
                for k in range(1, 4):
                    stage2(b, k).wait_recv()
                    value = value + quarter[b, k - 1].astype(F32)
                value = value * scale
                direct_out[b] = value.astype(BF16)
                if b < 5:
                    turned_out[b] = value.T.astype(BF16)
            when_active(b, finish)
            send_direct(b, 0)
            if b < 5:
                send_turned(b, 0)

    @pl.when(inner)
    def _():
        for c in range(CHUNKS):
            in_copy(c).wait_recv()

    reduce_blocks((5, 1))

    @pl.when(inner)
    def _():
        for c in range(CHUNKS):
            keep_copy(c).wait_recv()
            out_copy(c).wait_recv()

    reduce_blocks((3, 0, 2, 4))

    g = t // 2
    same_side = (p < 2) == (g < 2)
    cross = jnp.logical_not(same_side)
    has_direct = cross | (p == g) | outer
    direct_from = jnp.where(p == g, p, inner_of)
    has_turned = cross | ((p != g) & inner)
    turned_from = jnp.where(cross, far_in_of, inner_of)

    @pl.when(has_direct)
    def _():
        for uu in range(4):
            @pl.when(jnp.logical_not((direct_from == p) & (2 * uu + v == t)))
            def _():
                remote(direct_out.at[0], direct.at[pl.ds(uu * 128, 128), :], d_send.at[0],
                       d_recv.at[uu], (p, t)).wait_recv()
        gram_ref[...] = direct[...].astype(F32)

    @pl.when(has_turned)
    def _():
        for vv in range(2):
            for cc in range(2):
                @pl.when(jnp.logical_not((turned_from == p) & (2 * (2 * v + cc) + vv == t)))
                def _():
                    remote(turned_out.at[0], turned.at[vv * 2 + cc], t_send.at[0],
                           t_recv.at[vv * 2 + cc], (p, t)).wait_recv()

    for vv in range(2):
        for cc in range(2):
            rr, ll = slice(vv * 256, vv * 256 + 256), slice(cc * 128, cc * 128 + 128)

            @pl.when(has_turned & has_direct)
            def _():
                gram_ref[rr, ll] += turned[vv * 2 + cc].astype(F32)

            @pl.when(has_turned & jnp.logical_not(has_direct))
            def _():
                gram_ref[rr, ll] = turned[vv * 2 + cc].astype(F32)

    for b in range(6):
        def sent(b=b):
            stage1(b).wait_send()
            for k in range(1, 4):
                stage2(b, k).wait_send()
        when_active(b, sent)
        send_direct(b, 1)
        if b < 5:
            send_turned(b, 1)
    for side, sends, _, to in sides:
        @pl.when(sends)
        def _():
            dif_copy(side, to).wait_send()
            for c in range(CHUNKS):
                s_copy(side, to, c).wait_send()
                m_copy(side, to, c).wait_send()

    @pl.when(inner)
    def _():
        for c in range(CHUNKS):
            in_copy(c).wait_send()
            out_copy(c).wait_send()

    @pl.when(outer)
    def _():
        for c in range(CHUNKS - 2):
            away_copy(c).wait_send()
        for c in range(2, CHUNKS):
            keep_copy(c).wait_send()
    write_out.wait()


def slab(sensitivity, diffusivity, total_cells):
    rows, layers, width, ny = sensitivity.shape
    cells = width * ny
    dma = pltpu.SemaphoreType.DMA
    halo = layers * HALF * ny
    return pl.pallas_call(
        lambda *refs: slab_kernel(1.0 / total_cells, *refs),
        out_shape=[
            jax.ShapeDtypeStruct(sensitivity.shape, BF16),
            jax.ShapeDtypeStruct((512, 256), F32),
        ],
        in_specs=[pl.BlockSpec(memory_space=pltpu.VMEM)] * 2,
        out_specs=[pl.BlockSpec(memory_space=pl.ANY), pl.BlockSpec(memory_space=pltpu.VMEM)],
        scratch_shapes=[
            pltpu.VMEM((layers, rows * width, ny), F32),
            pltpu.VMEM((layers, rows, cells), BF16),
            pltpu.VMEM(sensitivity.shape, BF16),
            pltpu.VMEM((layers, BLOCK * width, ny), F32),
            pltpu.VMEM((rows, cells), BF16),
            pltpu.VMEM((rows, cells), BF16),
            pltpu.VMEM((rows, cells), BF16),
            pltpu.VMEM((rows, cells), BF16),
            pltpu.VMEM((2, rows, halo), BF16),
            pltpu.VMEM((2, rows, halo), BF16),
            pltpu.VMEM((2, layers, rows, HALF * ny), BF16),
            pltpu.VMEM((2, layers, width, ny), F32),
            pltpu.VMEM((layers, width + 16, ny), F32),
            pltpu.VMEM((6, layers, width + 8, ny), F32),
            pltpu.VMEM((6, 512, 256), BF16),
            pltpu.VMEM((6, 512, 256), F32),
            pltpu.VMEM((6, 512, 256), BF16),
            pltpu.VMEM((6, 512, 256), BF16),
            pltpu.VMEM((6, 3, 128, 256), BF16),
            pltpu.VMEM((6, 128, 256), BF16),
            pltpu.VMEM((6, 256, 128), BF16),
            pltpu.VMEM((512, 256), BF16),
            pltpu.VMEM((4, 256, 128), BF16),
            dma((2,)), dma((2,)),
            dma((2, CHUNKS)), dma((2, CHUNKS)),
            dma((2, CHUNKS)), dma((2, CHUNKS)),
            dma((CHUNKS,)), dma((CHUNKS,)),
            dma((CHUNKS,)), dma((CHUNKS,)),
            dma((CHUNKS,)), dma((CHUNKS,)),
            dma((CHUNKS,)), dma((CHUNKS,)),
            dma((1,)),
            dma((6,)), dma((6,)), dma((6, 3)), dma((6, 3)), dma((6,)), dma((6,)), dma((4,)), dma((4,)),
        ],
        compiler_params=pltpu.CompilerParams(
            collective_id=0, has_side_effects=True, vmem_limit_bytes=58 * 1024 * 1024
        ),
        cost_estimate=pl.CostEstimate(flops=0, bytes_accessed=50_000_000, transcendentals=0),
        name="slab",
    )(sensitivity, diffusivity)


def ring(field, total_cells):
    rows = field.shape[0]
    count = lax.axis_size("dp")
    pos = lax.axis_index("dp")
    pairs = [(s, (s + 1) % count) for s in range(count)]
    block = jnp.zeros((rows, rows * count), F32)

    def add(block, panel, source):
        return lax.dynamic_update_slice(block, gram_dot(field, panel), (jnp.int32(0), source * rows))

    block = add(block, field, pos)

    def turn(i, carry):
        block, panel = carry
        panel = lax.ppermute(panel, "dp", pairs)
        return add(block, panel, (pos - i) % count), panel

    block, _ = lax.fori_loop(1, count, turn, (block, field))
    cols = block.shape[1] // lax.axis_size("tile")
    own = lax.psum_scatter(block.astype(BF16), "tile", scatter_dimension=1, tiled=True)
    return own.astype(F32) / total_cells


def shards(sensitivity, diffusivity):
    rows, layers, width, ny = sensitivity.shape
    total_cells = layers * width * ny * lax.axis_size("tile")
    if lax.axis_size("dp") == 4 and lax.axis_size("tile") == 8 and sensitivity.shape == (512, 2, 16, 128):
        return slab(sensitivity, diffusivity, total_cells)
    coeff = coefficients(diffusivity)
    flat = sensitivity.reshape(rows, layers * width * ny)
    (middle,) = two_steps(flat, *first_halo(sensitivity), coeff, width, False)
    (smoothed,) = two_steps(middle, *flat_halo(middle, width), coeff, width, False)
    return smoothed.reshape(sensitivity.shape), ring(middle, total_cells)


def solution(mesh):
    in_specs = (P("dp", None, "tile", None), P(None, "tile", None))
    out_specs = (P("dp", None, "tile", None), P("dp", "tile"))
    return jax.shard_map(shards, mesh=mesh, in_specs=in_specs, out_specs=out_specs, check_vma=False)
```

```python
import jax
import jax.numpy as jnp
from jax import lax
from jax.experimental import pallas as pl
from jax.experimental.pallas import tpu as pltpu
from jax.sharding import PartitionSpec as P

STEPS = 4
HALF = 2
MESH = pl.DeviceIdType.MESH
F32 = jnp.float32
BF16 = jnp.bfloat16


def neighbours(block, dim, width, axis="tile"):
    count = lax.axis_size(axis)
    forward = [(i, i + 1) for i in range(count - 1)]
    backward = [(t, s) for s, t in forward]
    low = lax.ppermute(
        lax.slice_in_dim(block, block.shape[dim] - width, None, axis=dim), axis, forward
    )
    high = lax.ppermute(lax.slice_in_dim(block, 0, width, axis=dim), axis, backward)
    return low, high


def extended(block, dim, width):
    low, high = neighbours(block, dim, width)
    return jnp.concatenate([low, block, high], axis=dim)


def coefficients(diffusivity):
    layers, width, ny = diffusivity.shape
    d = extended(diffusivity, 1, HALF)
    tile, tiles = lax.axis_index("tile"), lax.axis_size("tile")
    c = d[:, 1:-1]
    xm = 0.5 * (c + d[:, :-2])
    xp = 0.5 * (c + d[:, 2:])
    cp = jnp.pad(c, ((1, 1), (0, 0), (0, 0)))
    lm = 0.5 * (c + cp[:-2])
    lp = 0.5 * (c + cp[2:])
    cy = jnp.pad(c, ((0, 0), (0, 0), (1, 1)))
    ym = 0.5 * (c + cy[:, :, :-2])
    yp = 0.5 * (c + cy[:, :, 2:])
    a0 = 1.0 - (xm + xp + lm + lp + ym + yp)
    lay = jnp.arange(layers)[:, None, None]
    col = jnp.arange(ny)[None, None, :]
    other = jnp.where(lay == 0, lp, lm)
    ym = jnp.where(col == 0, 0.0, ym)
    yp = jnp.where(col == ny - 1, 0.0, yp)
    x = jnp.arange(width + 2)[None, :, None]
    inside = ((x > 0) | (tile > 0)) & ((x < width + 1) | (tile < tiles - 1))
    stack = jnp.where(inside[None], jnp.stack([a0, xm, xp, other, ym, yp]), 0.0)
    return stack.reshape(6, layers * (width + 2), ny)


def smooth_kernel(width, split, main_ref, low_ref, high_ref, coeff_ref, out_ref, *halves):
    lanes = 128
    half = width * lanes

    def load(layer, x):
        if x < HALF:
            at = (layer * HALF + x) * lanes
            return low_ref[:, at : at + lanes].astype(F32)
        if x >= width + HALF:
            at = (layer * HALF + x - width - HALF) * lanes
            return high_ref[:, at : at + lanes].astype(F32)
        at = (layer * width + x - HALF) * lanes
        return main_ref[:, at : at + lanes].astype(F32)

    def step(read, layer, x, cx):
        at = layer * (width + 2) + cx
        w = [coeff_ref[i, at : at + 1, :] for i in range(6)]
        f = read(layer, x)
        total = w[0] * f + w[1] * read(layer, x - 1) + w[2] * read(layer, x + 1)
        total = total + w[3] * read(1 - layer, x)
        total = total + w[4] * pltpu.roll(f, 1, 1)
        return total + w[5] * pltpu.roll(f, lanes - 1, 1)

    first = {}

    def read_first(layer, x):
        if (layer, x) not in first:
            first[layer, x] = step(load, layer, x, x - 1)
        return first[layer, x]

    for x in range(HALF, width + HALF):
        for layer in range(2):
            value = step(read_first, layer, x, x - 1)
            at = (layer * width + x - HALF) * lanes
            out_ref[:, at : at + lanes] = value.astype(BF16)
    if split:
        away_ref, keep_ref = halves
        left = 2 * lax.axis_index("dp") < lax.axis_size("dp")

        @pl.when(left)
        def _():
            away_ref[...] = out_ref[:, :half]
            keep_ref[...] = out_ref[:, half:]

        @pl.when(jnp.logical_not(left))
        def _():
            away_ref[...] = out_ref[:, half:]
            keep_ref[...] = out_ref[:, :half]


def two_steps(main, low, high, coeff, width, split):
    rows, cells = main.shape
    block = 32
    outs = [cells] + ([cells // 2] * 2 if split else [])
    return pl.pallas_call(
        lambda *refs: smooth_kernel(width, split, *refs),
        out_shape=[jax.ShapeDtypeStruct((rows, n), BF16) for n in outs],
        grid=(rows // block,),
        in_specs=[
            pl.BlockSpec((block, cells), lambda i: (i, 0)),
            pl.BlockSpec((block, low.shape[1]), lambda i: (i, 0)),
            pl.BlockSpec((block, high.shape[1]), lambda i: (i, 0)),
            pl.BlockSpec(coeff.shape, lambda i: (0, 0, 0)),
        ],
        out_specs=[pl.BlockSpec((block, n), lambda i: (i, 0)) for n in outs],
        cost_estimate=pl.CostEstimate(
            flops=rows * cells * 24, bytes_accessed=rows * cells * 8, transcendentals=0
        ),
        name="two_steps",
    )(main, low, high, coeff)


def exchange(tops, bottoms):
    count = lax.axis_size("tile")
    forward = [(i, i + 1) for i in range(count - 1)]
    low = lax.ppermute(tops, "tile", forward)
    high = lax.ppermute(bottoms, "tile", [(t, s) for s, t in forward])
    return low, high


def flat_halo(flat, width):
    n = width * 128
    w = HALF * 128
    tops = jnp.concatenate([flat[:, n - w : n], flat[:, 2 * n - w :]], axis=1)
    bottoms = jnp.concatenate([flat[:, :w], flat[:, n : n + w]], axis=1)
    return exchange(tops, bottoms)


def first_halo(block):
    rows, width = block.shape[0], block.shape[2]
    return exchange(
        block[:, :, width - HALF :].reshape(rows, -1), block[:, :, :HALF].reshape(rows, -1)
    )


def gram_dot(a, b):
    return lax.dot_general(a, b, (((1,), (1,)), ((), ())), preferred_element_type=F32)


def mix(width, load, store, coeff_ref):
    lanes = 128
    loaded, first = {}, {}

    def read(layer, x):
        if (layer, x) not in loaded:
            loaded[layer, x] = load(layer, x)
        return loaded[layer, x]

    def step(source, layer, x, cx):
        w = [coeff_ref[i, layer, cx : cx + 1, :] for i in range(6)]
        f = source(layer, x)
        total = w[0] * f + w[1] * source(layer, x - 1) + w[2] * source(layer, x + 1)
        total = total + w[3] * source(1 - layer, x)
        total = total + w[4] * pltpu.roll(f, 1, 1)
        return total + w[5] * pltpu.roll(f, lanes - 1, 1)

    def read_first(layer, x):
        if (layer, x) not in first:
            first[layer, x] = step(read, layer, x, x - 1)
        return first[layer, x]

    for x in range(HALF, width + HALF):
        for layer in range(2):
            store(layer, x - HALF, step(read_first, layer, x, x - 1))


def make_coefficients(tile, tiles, width, ny, d_ref, low_ref, high_ref, ext_ref, coeff_ref):
    base = 8
    for layer in range(2):
        ext_ref[layer, base : base + width, :] = d_ref[layer]

        @pl.when(tile > 0)
        def _():
            ext_ref[layer, base - HALF : base, :] = low_ref[layer, width - HALF : width, :]

        @pl.when(tile == 0)
        def _():
            ext_ref[layer, base - HALF : base, :] = jnp.zeros((HALF, ny), F32)

        @pl.when(tile < tiles - 1)
        def _():
            ext_ref[layer, base + width : base + width + HALF, :] = high_ref[layer, 0:HALF, :]

        @pl.when(tile == tiles - 1)
        def _():
            ext_ref[layer, base + width : base + width + HALF, :] = jnp.zeros((HALF, ny), F32)

    n = width + 2
    at = base - 1
    row = lax.broadcasted_iota(jnp.int32, (n, ny), 0)
    col = lax.broadcasted_iota(jnp.int32, (n, ny), 1)
    inside = ((row > 0) | (tile > 0)) & ((row < n - 1) | (tile < tiles - 1))
    for layer in range(2):
        c = ext_ref[layer, at : at + n, :]
        xm = 0.5 * (c + ext_ref[layer, at - 1 : at - 1 + n, :])
        xp = 0.5 * (c + ext_ref[layer, at + 1 : at + 1 + n, :])
        other = 0.5 * (c + ext_ref[1 - layer, at : at + n, :])
        ym = 0.5 * (c + jnp.where(col == 0, 0.0, pltpu.roll(c, 1, 1)))
        yp = 0.5 * (c + jnp.where(col == ny - 1, 0.0, pltpu.roll(c, ny - 1, 1)))
        a0 = 1.0 - (xm + xp + other + 0.5 * c + ym + yp)
        ym = jnp.where(col == 0, 0.0, ym)
        yp = jnp.where(col == ny - 1, 0.0, yp)
        for i, value in enumerate([a0, xm, xp, other, ym, yp]):
            coeff_ref[i, layer, 0:n, :] = jnp.where(inside, value, 0.0)


UNITS = 8
BLOCK = 32
PART = 256


def slab_kernel(scale, s_hbm, d_ref, native, gram_ref, *scratch):
    (s_ref, s32, m, mixed, near_away, near_keep, far_in, far_out, s_out, s_halo, m_halo,
     d_halo, d_ext, coeff, direct, turned, direct_rest, turned_rest) = scratch[:18]
    (load_sem, dif_send, dif_recv, sh_send, sh_recv, mh_send, mh_recv, aw_send, aw_recv,
     kp_send, kp_recv, fi_send, fi_recv, fo_send, fo_recv, rd_send, rd_recv, place_send,
     d_recv, t_recv, rest_recv) = scratch[18:39]
    buffers = scratch[39:]
    rows, width, ny = s_ref.shape[0], s_ref.shape[2], s_ref.shape[3]
    unit = rows // UNITS
    p = lax.axis_index("dp")
    t = lax.axis_index("tile")
    tiles = 8
    u, v = t // 2, t % 2
    inner = (p == 1) | (p == 2)
    outer = jnp.logical_not(inner)
    side = jnp.where(p < 2, 0, 1)
    away = side
    keep = 1 - away
    outer_of = jnp.where(p < 2, 0, 3)
    inner_of = jnp.where(p < 2, 1, 2)
    far_in_of = 3 - inner_of
    far_out_of = 3 - outer_of

    def remote(src, dst, send, recv, to):
        return pltpu.make_async_remote_copy(
            src_ref=src, dst_ref=dst, send_sem=send, recv_sem=recv, device_id=to,
            device_id_type=MESH)

    def span(c, n=1):
        return pl.ds(pl.multiple_of(c * unit, unit), n * unit)

    def load_copy(c):
        return pltpu.make_async_copy(s_hbm.at[span(c)], s_ref.at[span(c)], load_sem.at[c])

    for c in range(UNITS):
        load_copy(c).start()

    barrier = pltpu.get_barrier_semaphore()

    def greet(n, _):
        @pl.when(n != p * tiles + t)
        def _():
            pl.semaphore_signal(barrier, inc=1, device_id=(n // tiles, n % tiles), device_id_type=MESH)
        return 0

    lax.fori_loop(0, 32, greet, 0)

    sides = [(0, t < tiles - 1, t > 0, t + 1), (1, t > 0, t < tiles - 1, t - 1)]

    def dif_copy(way, to):
        return remote(d_ref, d_halo.at[way], dif_send.at[way], dif_recv.at[way], (p, to))

    def s_copy(way, to, c):
        return remote(s_out.at[way, span(c), :], s_halo.at[way, span(c), :], sh_send.at[way, c],
                      sh_recv.at[way, c], (p, to))

    def m_copy(way, to, c):
        w = HALF * ny
        cols = pl.ds(width * ny - w, w) if way == 0 else pl.ds(0, w)
        return remote(m.at[:, span(c), cols], m_halo.at[way, :, span(c), :], mh_send.at[way, c],
                      mh_recv.at[way, c], (p, to))

    def unpack(c):
        load_copy(c).wait()

        def body(i, _):
            i = c * (unit // BLOCK) + i
            at = pl.ds(pl.multiple_of(i * BLOCK, BLOCK), BLOCK)
            n = BLOCK * width
            for layer in range(2):
                value = s_ref[at, layer].astype(F32)
                s32[layer, pl.ds(pl.multiple_of(i * n, n), n), :] = value.reshape(n, ny)
                for h in range(HALF):
                    for way, x in ((0, width - HALF + h), (1, h)):
                        cols = slice((layer * HALF + h) * ny, (layer * HALF + h + 1) * ny)
                        s_out[way, at, cols] = s32[
                            layer, pl.ds(i * n + x, BLOCK, stride=width), :].astype(BF16)
            return 0

        lax.fori_loop(0, unit // BLOCK, body, 0)

    def send_s(c):
        for way, sends, _, to in sides:
            pl.when(sends)(lambda way=way, to=to: s_copy(way, to, c).start())

    ahead = 2
    unpack(0)
    pl.semaphore_wait(barrier, 31)
    for way, sends, _, to in sides:
        pl.when(sends)(lambda way=way, to=to: dif_copy(way, to).start())
    send_s(0)

    def first_units(c, _):
        unpack(c)
        send_s(c)
        return 0

    lax.fori_loop(1, ahead, first_units, 0)

    for way, sends, gets, to in sides:
        @pl.when(gets)
        def _():
            dif_copy(way, to).wait_recv()

        @pl.when(jnp.logical_not(gets))
        def _():
            s_halo[way] = jnp.zeros(s_halo.shape[1:], BF16)
            m_halo[way] = jnp.zeros(m_halo.shape[1:], BF16)

    make_coefficients(t, tiles, width, ny, d_ref, d_halo.at[0], d_halo.at[1], d_ext, coeff)

    def away_copy(c):
        return remote(m.at[away, span(c), :], near_away.at[span(c), :], aw_send.at[c],
                      aw_recv.at[c], (inner_of, t))

    def keep_copy(c):
        return remote(m.at[keep, span(c), :], near_keep.at[span(c), :], kp_send.at[c],
                      kp_recv.at[c], (inner_of, t))

    def in_copy(c):
        return remote(m.at[away, span(c), :], far_in.at[span(c), :], fi_send.at[c],
                      fi_recv.at[c], (far_in_of, t))

    def out_copy(c):
        return remote(near_away.at[span(c), :], far_out.at[span(c), :], fo_send.at[c],
                      fo_recv.at[c], (far_in_of, t))

    def block_rows(c, i):
        i = c * (unit // BLOCK) + i
        return i, pl.ds(pl.multiple_of(i * BLOCK, BLOCK), BLOCK)

    def first_half(c, _):
        @pl.when(c + ahead < UNITS)
        def _():
            unpack(c + ahead)
            send_s(c + ahead)

        for way, _, gets, to in sides:
            pl.when(gets)(lambda way=way, to=to: s_copy(way, to, c).wait_recv())

        def body(i, _):
            i, at = block_rows(c, i)

            def load(layer, x):
                if HALF <= x < width + HALF:
                    return s32[layer, pl.ds(i * BLOCK * width + x - HALF, BLOCK, stride=width), :]
                way, h = (0, x) if x < HALF else (1, x - width - HALF)
                cols = slice((layer * HALF + h) * ny, (layer * HALF + h + 1) * ny)
                return s_halo[way, at, cols].astype(F32)

            def store(layer, x, value):
                m[layer, at, x * ny : (x + 1) * ny] = value.astype(BF16)

            mix(width, load, store, coeff)
            return 0

        lax.fori_loop(0, unit // BLOCK, body, 0)
        for way, sends, _, to in sides:
            pl.when(sends)(lambda way=way, to=to: m_copy(way, to, c).start())
        pl.when(inner)(lambda: in_copy(c).start())
        pl.when(outer & (c < 4))(lambda: keep_copy(c).start())

        @pl.when(outer & (c == 4))
        def _():
            away_copy(0).start()
            away_copy(1).start()
        return 0

    lax.fori_loop(0, UNITS, first_half, 0)

    def second_half(c, _):
        for way, _, gets, to in sides:
            pl.when(gets)(lambda way=way, to=to: m_copy(way, to, c).wait_recv())

        def body(i, _):
            i, at = block_rows(c, i)

            def load(layer, x):
                if HALF <= x < width + HALF:
                    return m[layer, at, (x - HALF) * ny : (x - HALF + 1) * ny].astype(F32)
                way, h = (0, x) if x < HALF else (1, x - width - HALF)
                return m_halo[way, layer, at, h * ny : (h + 1) * ny].astype(F32)

            def store(layer, x, value):
                mixed[layer, pl.ds(x, BLOCK, stride=width), :] = value

            mix(width, load, store, coeff)
            for layer in range(2):
                native[at, layer] = mixed[layer].reshape(BLOCK, width, ny).astype(BF16)
            return 0

        lax.fori_loop(0, unit // BLOCK, body, 0)
        pl.when(outer & (c == 2))(lambda: keep_copy(4).start())
        pl.when(outer & (c == 4))(lambda: keep_copy(5).start())
        return 0

    lax.fori_loop(0, UNITS, second_half, 0)

    def scatter(r):
        stage, parts, _ = buffers[3 * r : 3 * r + 3]
        q = stage.shape[1] // 4
        for k in range(1, tiles):
            to = (t + k) % tiles
            src = stage.at[:, pl.ds(pl.multiple_of(to // 2 * q, q), q),
                           pl.ds(pl.multiple_of(to % 2 * PART, PART), PART)]
            remote(src, parts.at[k - 1], rd_send.at[r], rd_recv.at[r], (p, to)).start()

    def all_parts(r):
        parts = buffers[3 * r + 1]
        return remote(parts, parts, rd_send.at[r], rd_recv.at[r], (p, t))

    def placement(r, i):
        start, row_group, col_groups, rest = rounds[r]
        piece = buffers[3 * r + 2]
        col_group = col_groups[i]
        q = piece.shape[1]
        row = start + u * q
        half = row // 256
        if rest:
            d_dst = direct_rest.at[pl.ds(pl.multiple_of(u * q, q), q), :]
            t_dst = turned_rest.at[pl.ds(pl.multiple_of(u * q, q), q),
                                   pl.ds(pl.multiple_of(v * PART, PART), PART)]
            sems = rest_recv.at[0], rest_recv.at[1]
        else:
            d_dst = direct.at[side, pl.ds(pl.multiple_of(row, q), q), :]
            t_dst = turned.at[side, pl.ds(pl.multiple_of(row - half * 256, q), q),
                              pl.ds(pl.multiple_of(v * PART, PART), PART)]
            sems = d_recv.at[side], t_recv.at[side]
        todo = [(d_dst, sems[0], row_group, 2 * col_group + v)]
        if r > 0:
            todo.append((t_dst, sems[1], col_group, 2 * row_group + half))
        for n, (dst, sem, dp, dt) in enumerate(todo):
            yield (dp == p) & (dt == t), piece.at[i], dst, place_send.at[r, i, n], sem, (dp, dt)

    def gather(r):
        stage, parts, piece = buffers[3 * r : 3 * r + 3]
        q = piece.shape[1]
        all_parts(r).wait_recv()
        for i in range(stage.shape[0]):
            value = stage[i, pl.ds(pl.multiple_of(u * q, q), q),
                          pl.ds(pl.multiple_of(v * PART, PART), PART)].astype(F32)
            for k in range(tiles - 1):
                value = value + parts[k, i].astype(F32)
            piece[i] = (value * scale).astype(BF16)
            for mine, src, dst, send, recv, to in placement(r, i):
                @pl.when(mine)
                def _():
                    dst[...] = src[...]

                @pl.when(jnp.logical_not(mine))
                def _():
                    remote(src, dst, send, recv, to).start()

    def settle(r):
        all_parts(r).wait_send()
        for i in range(buffers[3 * r].shape[0]):
            for mine, src, dst, send, recv, to in placement(r, i):
                @pl.when(jnp.logical_not(mine))
                def _():
                    remote(src, dst, send, recv, to).wait_send()

    pair = [inner_of, outer_of]
    rounds = [
        (0, p, [p], False),
        (0, far_in_of, [inner_of], False),
        (0, outer_of, [far_in_of, inner_of], False),
        (256, outer_of, [far_in_of, inner_of], False),
        (384, outer_of, [far_in_of, inner_of], False),
        (448, outer_of, [far_in_of, inner_of], False),
        (0, far_out_of, pair, False),
        (128, far_out_of, pair, False),
        (256, far_out_of, pair, False),
        (384, far_out_of, pair, False),
        (448, far_out_of, pair, False),
        (384, outer_of, [far_out_of], True),
    ]

    def from_keep(r):
        start, stage = rounds[r][0], buffers[3 * r]
        at = slice(start, start + stage.shape[1])
        stage[0] = gram_dot(near_keep[at, :], far_in[...]).astype(BF16)
        stage[1] = (gram_dot(near_keep[at, :], m[keep]) + gram_dot(near_away[at, :], m[away])).astype(BF16)
        scatter(r)

    def from_out(r):
        start, stage = rounds[r][0], buffers[3 * r]
        at = slice(start, start + stage.shape[1])
        for c in range(start // unit, (start + stage.shape[1]) // unit):
            out_copy(c).wait_recv()
        stage[0] = gram_dot(far_out[at, :], m[keep]).astype(BF16)
        stage[1, :, 0:384] = gram_dot(far_out[at, :], near_keep[0:384, :]).astype(BF16)
        stage[1, :, 384:512] = jnp.zeros((stage.shape[1], 128), BF16)
        scatter(r)

    def take_keep(first, last):
        for c in range(first, last):
            keep_copy(c).wait_recv()

    def forward(c):
        away_copy(c).wait_recv()
        out_copy(c).start()

    def own_block():
        buffers[0][0] = (gram_dot(m[0], m[0]) + gram_dot(m[1], m[1])).astype(BF16)
        scatter(0)

    @pl.when(outer)
    def _():
        away_copy(2).start()
        away_copy(3).start()

    @pl.when(inner)
    def _():
        forward(0)
        forward(1)

    own_block()

    @pl.when(outer)
    def _():
        away_copy(1).wait_send()
        away_copy(4).start()
        away_copy(2).wait_send()
        away_copy(5).start()

    @pl.when(inner)
    def _():
        for c in range(UNITS):
            in_copy(c).wait_recv()
        buffers[3][0] = gram_dot(far_in[...], m[keep]).astype(BF16)
        scatter(1)

    gather(0)

    @pl.when(outer)
    def _():
        for c, (done, start) in enumerate([
            (away_copy(3), away_copy(6)), (away_copy(4), away_copy(7)),
            (away_copy(5), keep_copy(6)), (away_copy(6), keep_copy(7)),
        ]):
            done.wait_send()
            start.start()

    @pl.when(inner)
    def _():
        forward(2)
        forward(3)
        take_keep(0, 4)
        from_keep(2)
        gather(1)
        take_keep(4, 6)
        from_out(6)
        gather(2)
        forward(4)
        gather(6)
        forward(5)
        from_keep(3)
        from_out(7)
        gather(3)
        forward(6)
        gather(7)
        forward(7)
        from_out(8)
        gather(8)
        take_keep(6, 7)
        from_keep(4)
        from_out(9)
        gather(4)
        gather(9)
        take_keep(7, 8)
        from_keep(5)
        from_out(10)
        buffers[33][0] = gram_dot(near_keep[384:512, :], far_out[...]).astype(BF16)
        scatter(11)
        gather(5)
        gather(10)
        gather(11)

    g, h = t // 2, t % 2
    g_inner = (g == 1) | (g == 2)
    g_side = jnp.where(g < 2, 0, 1)
    cross = side != g_side
    both_ways = cross & (inner == g_inner)
    gram_ref[...] = jnp.zeros(gram_ref.shape, F32)
    for s in range(2):
        near = side == s
        has_direct = (near & (p == g)) | (near & (side == g_side) & (p != g) & outer) | (
            cross & (inner != g_inner) & outer) | (both_ways & jnp.logical_not(near))
        has_turned = (near & (side == g_side) & (p != g) & inner) | (
            cross & (inner != g_inner) & inner) | (both_ways & near)

        def arrive(buffer, sem, when, eighths):
            @pl.when(when)
            def _():
                n = buffer.shape[1] * eighths // 8
                part = buffer.at[s, 0:n, :]
                remote(part, part, sem.at[s], sem.at[s], (p, t)).wait_recv()

        own_cell = near & (p == g)
        arrive(direct, d_recv, own_cell, 6)
        arrive(direct, d_recv, has_direct & jnp.logical_not(own_cell), 8)
        through = near & inner & jnp.logical_not(g_inner)
        middle = near & both_ways & inner & (h == g // 2)
        arrive(turned, t_recv, through, 7)
        arrive(turned, t_recv, middle, 6)
        arrive(turned, t_recv, has_turned & jnp.logical_not(through | middle), 8)

        @pl.when(has_direct)
        def _():
            gram_ref[...] += direct[s].astype(F32)

        @pl.when(has_turned)
        def _():
            gram_ref[...] += turned[s].astype(F32).T

    corner = both_ways & outer

    @pl.when(corner)
    def _():
        remote(direct_rest, direct_rest, rest_recv.at[0], rest_recv.at[0], (p, t)).wait_recv()
        gram_ref[384:512, :] += direct_rest[...].astype(F32)

    @pl.when(corner & (h == 1))
    def _():
        remote(turned_rest, turned_rest, rest_recv.at[1], rest_recv.at[1], (p, t)).wait_recv()
        gram_ref[:, 128:256] += turned_rest[...].astype(F32).T

    settle(0)

    @pl.when(inner)
    def _():
        for r in range(1, len(rounds)):
            settle(r)
        for c in range(UNITS):
            in_copy(c).wait_send()
            out_copy(c).wait_send()

    @pl.when(outer)
    def _():
        away_copy(0).wait_send()
        away_copy(7).wait_send()
        for c in range(UNITS):
            keep_copy(c).wait_send()
    for way, sends, _, to in sides:
        @pl.when(sends)
        def _():
            dif_copy(way, to).wait_send()
            for c in range(UNITS):
                s_copy(way, to, c).wait_send()
                m_copy(way, to, c).wait_send()


ROUND_SHAPES = [
    (1, 512), (1, 512), (2, 256), (2, 128), (2, 64), (2, 64),
    (2, 128), (2, 128), (2, 128), (2, 64), (2, 64), (1, 128),
]


def write_kernel(native, gram, smoothed_ref, gram_ref, sem):
    first = pltpu.make_async_copy(native, smoothed_ref, sem.at[0])
    second = pltpu.make_async_copy(gram, gram_ref, sem.at[1])
    first.start()
    second.start()
    first.wait()
    second.wait()


def slab(sensitivity, diffusivity, total_cells):
    rows, layers, width, ny = sensitivity.shape
    cells = width * ny
    dma = pltpu.SemaphoreType.DMA
    halo = layers * HALF * ny
    buffers = []
    for n, r in ROUND_SHAPES:
        buffers.append(pltpu.VMEM((n, r, 2 * PART), BF16))
        buffers.append(pltpu.VMEM((7, n, r // 4, PART), BF16))
        buffers.append(pltpu.VMEM((n, r // 4, PART), BF16))
    count = len(ROUND_SHAPES)
    out_shape = [
        jax.ShapeDtypeStruct(sensitivity.shape, BF16),
        jax.ShapeDtypeStruct((512, 256), F32),
    ]
    results = pl.pallas_call(
        lambda *refs: slab_kernel(1.0 / total_cells, *refs),
        out_shape=out_shape,
        in_specs=[pl.BlockSpec(memory_space=pl.ANY), pl.BlockSpec(memory_space=pltpu.VMEM)],
        out_specs=[pl.BlockSpec(memory_space=pltpu.VMEM)] * 2,
        scratch_shapes=[
            pltpu.VMEM(sensitivity.shape, BF16),
            pltpu.VMEM((layers, rows * width, ny), F32),
            pltpu.VMEM((layers, rows, cells), BF16),
            pltpu.VMEM((layers, BLOCK * width, ny), F32),
            pltpu.VMEM((rows, cells), BF16),
            pltpu.VMEM((rows, cells), BF16),
            pltpu.VMEM((rows, cells), BF16),
            pltpu.VMEM((rows, cells), BF16),
            pltpu.VMEM((2, rows, halo), BF16),
            pltpu.VMEM((2, rows, halo), BF16),
            pltpu.VMEM((2, layers, rows, HALF * ny), BF16),
            pltpu.VMEM((2, layers, width, ny), F32),
            pltpu.VMEM((layers, width + 16, ny), F32),
            pltpu.VMEM((6, layers, width + 8, ny), F32),
            pltpu.VMEM((2, 512, 256), BF16),
            pltpu.VMEM((2, 256, 512), BF16),
            pltpu.VMEM((128, 256), BF16),
            pltpu.VMEM((128, 512), BF16),
            dma((UNITS,)), dma((2,)), dma((2,)),
            dma((2, UNITS)), dma((2, UNITS)),
            dma((2, UNITS)), dma((2, UNITS)),
            dma((UNITS,)), dma((UNITS,)),
            dma((UNITS,)), dma((UNITS,)),
            dma((UNITS,)), dma((UNITS,)),
            dma((UNITS,)), dma((UNITS,)),
            dma((count,)), dma((count,)), dma((count, 2, 2)), dma((2,)), dma((2,)), dma((2,)),
        ] + buffers,
        compiler_params=pltpu.CompilerParams(
            collective_id=0, has_side_effects=True, vmem_limit_bytes=48 * 1024 * 1024
        ),
        cost_estimate=pl.CostEstimate(flops=0, bytes_accessed=50_000_000, transcendentals=0),
        name="slab",
    )(sensitivity, diffusivity)
    return pl.pallas_call(
        write_kernel,
        out_shape=out_shape,
        in_specs=[pl.BlockSpec(memory_space=pl.ANY)] * 2,
        out_specs=[pl.BlockSpec(memory_space=pl.ANY)] * 2,
        scratch_shapes=[dma((2,))],
        compiler_params=pltpu.CompilerParams(vmem_limit_bytes=1024 * 1024),
        name="write",
    )(*results)


def ring(field, total_cells):
    rows = field.shape[0]
    count = lax.axis_size("dp")
    pos = lax.axis_index("dp")
    pairs = [(s, (s + 1) % count) for s in range(count)]
    block = jnp.zeros((rows, rows * count), F32)

    def add(block, panel, source):
        return lax.dynamic_update_slice(block, gram_dot(field, panel), (jnp.int32(0), source * rows))

    block = add(block, field, pos)

    def turn(i, carry):
        block, panel = carry
        panel = lax.ppermute(panel, "dp", pairs)
        return add(block, panel, (pos - i) % count), panel

    block, _ = lax.fori_loop(1, count, turn, (block, field))
    cols = block.shape[1] // lax.axis_size("tile")
    own = lax.psum_scatter(block.astype(BF16), "tile", scatter_dimension=1, tiled=True)
    return own.astype(F32) / total_cells


def shards(sensitivity, diffusivity):
    rows, layers, width, ny = sensitivity.shape
    total_cells = layers * width * ny * lax.axis_size("tile")
    if lax.axis_size("dp") == 4 and lax.axis_size("tile") == 8 and sensitivity.shape == (512, 2, 16, 128):
        return slab(sensitivity, diffusivity, total_cells)
    coeff = coefficients(diffusivity)
    flat = sensitivity.reshape(rows, layers * width * ny)
    (middle,) = two_steps(flat, *first_halo(sensitivity), coeff, width, False)
    (smoothed,) = two_steps(middle, *flat_halo(middle, width), coeff, width, False)
    return smoothed.reshape(sensitivity.shape), ring(middle, total_cells)


def solution(mesh):
    in_specs = (P("dp", None, "tile", None), P(None, "tile", None))
    out_specs = (P("dp", None, "tile", None), P("dp", "tile"))
    return jax.shard_map(shards, mesh=mesh, in_specs=in_specs, out_specs=out_specs, check_vma=False)
```
